32 devices in a mesh: groups: 2 (over x), seq: 16 (over z, y, core).
Axes of the slice: x: 2, y: 2, z: 4, core: 2. Of those that a mesh axis runs over, the one named last changes fastest.
Arguments:
- queries: bfloat16 [8192, 4096], P(('groups', 'seq')), parts along dimension 0, may hold values from -6 to 6
- key_rows: bfloat16 [8192, 2048], P(('groups', 'seq')), parts along dimension 0, may hold values from -6 to 6
- value_matrix: bfloat16 [8192, 2048], P(('groups', 'seq')), parts along dimension 0, may hold values from -6 to 6
Outputs:
- attended: bfloat16 [8192, 4096], P(('groups', 'seq')), parts along dimension 0
The draws below stay inside these ranges and needn't reach their ends.
There are 2 independent parts, one for each index of `groups`. The reference program is written for one: setup_inputs(seed, part) draws one part's arguments, and reference() takes and returns one part's arrays. A program takes and returns all parts, laid end to end along the dimension named above; each array names one. Nothing has to cross between parts.
All inputs are finite; a program needn't handle non-finite values.
Results may differ from the reference program's by a relative error of at most 0.0045.
Values may be sent and summed in bfloat16 or wider, within the bound.
No kernel may reach another device: no remote copies, remote signals or barrier semaphores. Data moves between devices by JAX's collectives and lax.ppermute only.
A program may use at most 64 MiB of HBM per device.

```python
import jax
import jax.numpy as jnp
from jax import lax

QUERY_HEADS = 32
KEY_VALUE_HEADS = 16
HEAD_WIDTH = 128
WINDOW = 1024
TOK_DEV = 256
SEQUENCE_LENGTH = 4096
REACH = 4
N_SEQ = 16


def draw_queries(key, part):
    own_key = jax.random.fold_in(key, 1)
    complete_shape = (SEQUENCE_LENGTH, QUERY_HEADS * HEAD_WIDTH)
    values_base = jnp.clip(jax.random.normal(own_key, complete_shape, jnp.float32), -6.0, 6.0)
    return values_base.astype(jnp.bfloat16)


def draw_key_rows(key, part):
    own_key = jax.random.fold_in(key, 2)
    complete_shape = (SEQUENCE_LENGTH, KEY_VALUE_HEADS * HEAD_WIDTH)
    values_base = jnp.clip(jax.random.normal(own_key, complete_shape, jnp.float32), -6.0, 6.0)
    return values_base.astype(jnp.bfloat16)


def block_levels(key, extent, pieces, smallest, high):
    loudness, own = 1.0, jax.random.fold_in(key, 6)
    for dim, parts in pieces:
        heights = jnp.exp(jax.random.uniform(jax.random.fold_in(own, dim), (parts,), jnp.float32, smallest / len(pieces), high / len(pieces)))
        loudness = loudness * jnp.repeat(heights, extent[dim] // parts).reshape([-1 if axis == dim else 1 for axis in range(len(extent))])
    return loudness


def bell_draw(key, dims, width, reach, split=(), kind=jnp.bfloat16):
    entries = jax.random.normal(key, dims, jnp.float32) * width
    if len(split) > 0:
        entries = block_levels(key, dims, split, -0.22, 0.18) * entries
    return jnp.clip(entries, min=-reach, max=reach).astype(kind)


def setup_inputs(seed: int = 0, part: int = 0) -> dict:
    key_of = jax.random.split(jax.random.key(seed), 4)
    part_keys = jax.random.split(jax.random.fold_in(key_of[3], part), 4)
    queries = draw_queries(jax.random.fold_in(jax.random.fold_in(key_of[3], part), 71), part)
    key_rows = draw_key_rows(jax.random.fold_in(jax.random.fold_in(key_of[3], part), 71), part)
    value_matrix = bell_draw(part_keys[2], (SEQUENCE_LENGTH, KEY_VALUE_HEADS * HEAD_WIDTH), 1.0, 6.0, ((0, 16),))
    return {"queries": queries, "key_rows": key_rows, "value_matrix": value_matrix}


score_scale = 168.0 ** -0.5
masked_value = -1.0e30


def attend_window(query_block, key_win, value_win, query_pos, key_pos):
    query_groups = QUERY_HEADS // KEY_VALUE_HEADS
    length = query_block.shape[0]
    visible = (key_pos[None, :] <= query_pos[:, None]) & (key_pos[None, :] > query_pos[:, None] - WINDOW) & (key_pos[None, :] >= 0)

    def head_count_ratio(head_index, output):
        query_head = lax.dynamic_slice_in_dim(query_block, head_index * query_groups * HEAD_WIDTH, query_groups * HEAD_WIDTH, 1).reshape(length, query_groups, HEAD_WIDTH)
        key_head = lax.dynamic_slice_in_dim(key_win, head_index * HEAD_WIDTH, HEAD_WIDTH, 1)
        value_head = lax.dynamic_slice_in_dim(value_win, head_index * HEAD_WIDTH, HEAD_WIDTH, 1)
        raw_scores = jnp.einsum("tgd,kd->gtk", query_head.astype(jnp.float32), key_head.astype(jnp.float32)) * score_scale
        raw_scores = jnp.where(visible[None], raw_scores, masked_value)
        row_max = jnp.max(raw_scores, axis=2)
        weights_full = jnp.where(visible[None], jnp.exp(raw_scores - row_max[:, :, None]), 0.0)
        row_total = jnp.sum(weights_full, axis=2)
        weights = weights_full.astype(jnp.bfloat16)
        weighted = jnp.einsum("gtk,kd->tgd", weights.astype(jnp.float32), value_head.astype(jnp.float32))
        result = weighted / jnp.transpose(row_total)[:, :, None]
        result = result.reshape(length, query_groups * HEAD_WIDTH).astype(jnp.bfloat16)
        return lax.dynamic_update_slice_in_dim(output, result, head_index * query_groups * HEAD_WIDTH, 1)

    return lax.fori_loop(0, KEY_VALUE_HEADS, head_count_ratio, jnp.zeros(query_block.shape, jnp.bfloat16))


def reference(queries, key_rows, value_matrix):
    length = TOK_DEV
    padding = REACH * length
    span = (REACH + 1) * length
    key_pad = jnp.concatenate([jnp.zeros((padding, key_rows.shape[1]), key_rows.dtype), key_rows], axis=0)
    value_pad = jnp.concatenate([jnp.zeros((padding, value_matrix.shape[1]), value_matrix.dtype), value_matrix], axis=0)

    def one_block(block_index):
        start = (block_index * length).astype(jnp.int32)
        query_block = lax.dynamic_slice_in_dim(queries, start, length, 0)
        key_win = lax.dynamic_slice_in_dim(key_pad, start, span, 0)
        value_win = lax.dynamic_slice_in_dim(value_pad, start, span, 0)
        query_pos = start + jnp.arange(length, dtype=jnp.int32)
        key_pos = start - padding + jnp.arange(span, dtype=jnp.int32)
        return attend_window(query_block, key_win, value_win, query_pos, key_pos)

    blocks_out = lax.map(one_block, jnp.arange(N_SEQ, dtype=jnp.int32))
    return blocks_out.reshape(SEQUENCE_LENGTH, QUERY_HEADS * HEAD_WIDTH)
```

```python
import functools

import jax
import jax.numpy as jnp
from jax import lax
from jax.experimental import pallas as pl
from jax.experimental.pallas import tpu as pltpu
from jax.sharding import PartitionSpec as P

QUERY_HEADS = 32
KEY_VALUE_HEADS = 16
HEAD_WIDTH = 128
WINDOW = 1024
GROUP = QUERY_HEADS // KEY_VALUE_HEADS

score_scale = 168.0 ** (-0.5)
LOG2_E = 1.4426950408889634
masked_value = -1e30
ROWS = 64
CHUNKS = (5, 5, 4, 2)


def attend_kernel(block_ref, q_ref, own_ref, far_ref, mid_ref, pair1_ref, pair2_ref, *rest):
    o_ref = rest[-1]
    length = q_ref.shape[0]
    block = block_ref[0]
    odd = lax.rem(block, 2)

    def bias_of(back):
        return jnp.where(block >= back, 0.0, masked_value).astype(jnp.float32)

    far_bias = bias_of(4)
    biases = (0.0, bias_of(2), bias_of(3 - 2 * odd), bias_of(1 + 2 * odd))
    refs = (own_ref, far_ref, mid_ref, pair1_ref, pair2_ref)
    across = (((1,), (1,)), ((), ()))
    scale = score_scale * LOG2_E
    for start in range(0, length, ROWS):
        rows = slice(start, start + ROWS)
        query = jnp.concatenate(
            [q_ref[rows, g * HEAD_WIDTH : (g + 1) * HEAD_WIDTH] for g in range(GROUP)], axis=0
        )
        raw = [
            lax.dot_general(query, ref[0], across, preferred_element_type=jnp.float32)
            for ref in refs
        ]
        query_pos = lax.broadcasted_iota(jnp.int32, (ROWS, length), 0) + start
        key_pos = lax.broadcasted_iota(jnp.int32, (ROWS, length), 1)
        causal = jnp.concatenate([key_pos <= query_pos] * GROUP, axis=0)
        scores = [jnp.where(causal, raw[0], raw[1] + far_bias)] + raw[2:]
        row_max = functools.reduce(
            jnp.maximum,
            [jnp.max(s, axis=1, keepdims=True) + b for s, b in zip(scores, biases)],
        )
        weights = [jnp.exp2(s * scale + (b - row_max) * scale) for s, b in zip(scores, biases)]
        own_weights = jnp.where(causal, weights[0], 0.0)
        far_weights = jnp.where(causal, 0.0, weights[0])
        weights = [
            w.astype(jnp.bfloat16) for w in [own_weights, far_weights] + weights[1:]
        ]
        values = jnp.concatenate([ref[1] for ref in refs], axis=0)
        values = jnp.concatenate([values, jnp.ones_like(values)], axis=1)
        weighted = jnp.dot(
            jnp.concatenate(weights, axis=1), values, preferred_element_type=jnp.float32
        )
        result = weighted[:, :HEAD_WIDTH] / weighted[:, HEAD_WIDTH:]
        for g in range(GROUP):
            o_ref[rows, g * HEAD_WIDTH : (g + 1) * HEAD_WIDTH] = result[
                g * ROWS : (g + 1) * ROWS
            ].astype(o_ref.dtype)


def attend(block, queries, pieces, first, heads, output):
    length = queries.shape[0]
    kv_spec = pl.BlockSpec((2, length, HEAD_WIDTH), lambda h: (0, 0, h))
    q_spec = pl.BlockSpec((length, GROUP * HEAD_WIDTH), lambda h: (0, h + first))
    specs = [pl.BlockSpec(memory_space=pltpu.SMEM), q_spec] + [kv_spec] * len(pieces)
    args = [block, queries, *pieces]
    aliases = {}
    if output is not None:
        aliases = {len(args): 0}
        specs.append(pl.BlockSpec(memory_space=pl.ANY))
        args.append(output)
    keys = len(pieces) * length
    return pl.pallas_call(
        attend_kernel,
        name=f"attend_{first}",
        out_shape=jax.ShapeDtypeStruct(queries.shape, queries.dtype),
        grid=(heads,),
        in_specs=specs,
        out_specs=q_spec,
        input_output_aliases=aliases,
        compiler_params=pltpu.CompilerParams(vmem_limit_bytes=24 << 20),
        cost_estimate=pl.CostEstimate(
            flops=heads * GROUP * length * keys * HEAD_WIDTH * 4,
            transcendentals=heads * GROUP * length * WINDOW,
            bytes_accessed=heads * HEAD_WIDTH * length * 2 * (2 * len(pieces) + 2 * GROUP),
        ),
    )(*args)


def per_device(queries, key_rows, value_matrix):
    length = queries.shape[0]
    devices = lax.axis_size("seq")
    assert WINDOW == 4 * length and devices % 4 == 0
    far = [(i, i + 4) for i in range(devices - 4)]
    swap = [(i, i + 2 if i % 4 < 2 else i - 2) for i in range(devices)]
    pair = [(i, i ^ 1) for i in range(devices)]
    block = lax.axis_index("seq")
    upper = lax.rem(block, 4) >= 2
    odd = lax.rem(block, 2) == 1
    block = block.astype(jnp.int32).reshape(1)

    bounds = [0]
    for heads in CHUNKS:
        bounds.append(bounds[-1] + heads)
    assert bounds[-1] == KEY_VALUE_HEADS
    own = []
    for first, last in zip(bounds, bounds[1:]):
        columns = slice(first * HEAD_WIDTH, last * HEAD_WIDTH)
        own.append(jnp.stack([key_rows[:, columns], value_matrix[:, columns]]))
    from_far = [lax.ppermute(piece, "seq", far) for piece in own]
    output = None
    for chunk, heads in enumerate(CHUNKS):
        mine, distant = own[chunk], from_far[chunk]
        middle = lax.ppermute(jnp.where(upper, distant, mine), "seq", swap)
        pair1 = lax.ppermute(jnp.where(odd, distant, mine), "seq", pair)
        pair2 = lax.ppermute(middle, "seq", pair)
        output = attend(
            block, queries, (mine, distant, middle, pair1, pair2), bounds[chunk], heads, output
        )
    return output


def solution(mesh):
    return jax.shard_map(
        per_device,
        mesh=mesh,
        in_specs=(
            P(("groups", "seq"), None),
            P(("groups", "seq"), None),
            P(("groups", "seq"), None),
        ),
        out_specs=P(("groups", "seq"), None),
        check_vma=False,
    )
```

```python
import jax
import jax.numpy as jnp
from jax import lax
from jax.experimental import pallas as pl
from jax.experimental.pallas import tpu as pltpu
from jax.sharding import PartitionSpec as P


QUERY_HEADS = 32
KEY_VALUE_HEADS = 16
HEAD_WIDTH = 128
WINDOW = 1024
GROUP = QUERY_HEADS // KEY_VALUE_HEADS

score_scale = 168.0 ** (-0.5)
LOG2_E = 1.4426950408889634
masked_value = -1e30
CHUNKS = (4, 4, 4, 4)


def pack_kernel(_, key_ref, value_ref, out_ref):
    length = key_ref.shape[0]
    for head in range(out_ref.shape[0]):
        columns = slice(head * HEAD_WIDTH, (head + 1) * HEAD_WIDTH)
        out_ref[head, :length] = key_ref[:, columns]
        for start in range(0, length, HEAD_WIDTH):
            rows = slice(length + start, length + start + HEAD_WIDTH)
            out_ref[head, rows] = value_ref[start : start + HEAD_WIDTH, columns].T


def pack(flags, key_rows, value_matrix, first, heads):
    length = key_rows.shape[0]
    spec = pl.BlockSpec((length, heads * HEAD_WIDTH), lambda _: (0, first // heads))
    return pl.pallas_call(
        pack_kernel,
        out_shape=jax.ShapeDtypeStruct((heads, 2 * length, HEAD_WIDTH), key_rows.dtype),
        grid=(1,),
        in_specs=[pl.BlockSpec(memory_space=pltpu.SMEM), spec, spec],
        out_specs=pl.BlockSpec((heads, 2 * length, HEAD_WIDTH), lambda _: (0, 0, 0)),
        compiler_params=pltpu.CompilerParams(vmem_limit_bytes=8 << 20),
        cost_estimate=pl.CostEstimate(
            flops=0, transcendentals=0, bytes_accessed=8 * heads * length * HEAD_WIDTH
        ),
    )(flags, key_rows, value_matrix)


def attend_kernel(block_ref, q_ref, own_ref, far_ref, mid_ref, pair1_ref, pair2_ref, *rest):
    o_ref, *score_refs = rest[-5:-2]
    max_refs = rest[-2:]
    heads, length = own_ref.shape[0], q_ref.shape[0]
    block = block_ref[0]
    odd = lax.rem(block, 2)

    def bias_of(back):
        return jnp.where(block >= back, 0.0, masked_value).astype(jnp.float32)

    far_bias = bias_of(4)
    biases = (0.0, bias_of(2), bias_of(3 - 2 * odd), bias_of(1 + 2 * odd))
    others = (None, mid_ref, pair1_ref, pair2_ref)
    across = (((1,), (1,)), ((), ()))
    scale = score_scale * LOG2_E
    ones = jnp.ones((16, length), jnp.bfloat16)
    key_pos = lax.broadcasted_iota(jnp.int32, (length, length), 0)
    query_pos = lax.broadcasted_iota(jnp.int32, (length, length), 1)
    causal = key_pos <= query_pos

    def columns(head, g):
        return pl.ds(pl.multiple_of((head * GROUP + g) * HEAD_WIDTH, HEAD_WIDTH), HEAD_WIDTH)

    def score(head, g, part, row_max):
        query = q_ref[:, columns(head, g)]

        def product(ref):
            return lax.dot_general(
                ref[head, :length], query, across, preferred_element_type=jnp.float32
            )

        if part == 0:
            raw = jnp.where(causal, product(own_ref), product(far_ref) + far_bias)
        else:
            raw = product(others[part])
        score_refs[g][part * length : (part + 1) * length] = raw
        largest = jnp.max(raw.reshape(length // 8, 8, length), axis=0) + biases[part]
        return largest if row_max is None else jnp.maximum(row_max, largest)

    def keep_max(g, row_max):
        row_max = jnp.max(row_max, axis=0, keepdims=True) * scale
        max_refs[g][...] = jnp.broadcast_to(row_max, max_refs[g].shape)

    def weigh(head, g, part, total):
        shift = max_refs[g][0:1] - biases[part] * scale
        weights = jnp.exp2(score_refs[g][part * length : (part + 1) * length] * scale - shift)
        if part == 0:
            pieces = (
                (own_ref, jnp.where(causal, weights, 0.0)),
                (far_ref, jnp.where(causal, 0.0, weights)),
            )
        else:
            pieces = ((others[part], weights),)
        for ref, piece in pieces:
            values = jnp.concatenate(
                [
                    ref[head, length + start : length + start + HEAD_WIDTH]
                    for start in range(0, length, HEAD_WIDTH)
                ],
                axis=1,
            )
            product = jnp.dot(
                jnp.concatenate([values, ones], axis=0),
                piece.astype(jnp.bfloat16),
                preferred_element_type=jnp.float32,
            )
            total = product if total is None else total + product
        return total

    def finish(head, g, total):
        result = total[:HEAD_WIDTH] / total[HEAD_WIDTH : HEAD_WIDTH + 1]
        o_ref[:, columns(head, g)] = result.T.astype(o_ref.dtype)

    def overlap(head, g, next_head, next_g):
        row_max = total = None
        for part in range(4):
            row_max = score(next_head, next_g, part, row_max)
            total = weigh(head, g, part, total)
        keep_max(next_g, row_max)
        finish(head, g, total)

    row_max = None
    for part in range(4):
        row_max = score(0, 0, part, row_max)
    keep_max(0, row_max)

    def step(head, _):
        overlap(head, 0, head, 1)
        overlap(head, 1, jnp.minimum(head + 1, heads - 1), 0)
        return 0

    lax.fori_loop(0, heads, step, 0)


def attend(block, queries, pieces, first, heads, output):
    length = queries.shape[0]
    kv_spec = pl.BlockSpec((heads, 2 * length, HEAD_WIDTH), lambda _: (0, 0, 0))
    q_spec = pl.BlockSpec((length, heads * GROUP * HEAD_WIDTH), lambda _: (0, first // heads))
    specs = [pl.BlockSpec(memory_space=pltpu.SMEM), q_spec] + [kv_spec] * len(pieces)
    args = [block, queries, *pieces]
    aliases = {}
    if output is not None:
        aliases = {len(args): 0}
        specs.append(pl.BlockSpec(memory_space=pl.ANY))
        args.append(output)
    keys = len(pieces) * length
    return pl.pallas_call(
        attend_kernel,
        out_shape=jax.ShapeDtypeStruct(queries.shape, queries.dtype),
        grid=(1,),
        in_specs=specs,
        out_specs=q_spec,
        scratch_shapes=[pltpu.VMEM((WINDOW, length), jnp.float32)] * 2
        + [pltpu.VMEM((8, length), jnp.float32)] * 2,
        input_output_aliases=aliases,
        compiler_params=pltpu.CompilerParams(vmem_limit_bytes=16 << 20),
        cost_estimate=pl.CostEstimate(
            flops=heads * GROUP * length * keys * HEAD_WIDTH * 4,
            transcendentals=heads * GROUP * length * WINDOW,
            bytes_accessed=heads * HEAD_WIDTH * length * 2 * (2 * len(pieces) + 2 * GROUP),
        ),
    )(*args)


def per_device(queries, key_rows, value_matrix):
    length = queries.shape[0]
    devices = lax.axis_size("seq")
    assert WINDOW == 4 * length and devices % 4 == 0
    far = [(i, i + 4) for i in range(devices - 4)]
    swap = [(i, i + 2 if i % 4 < 2 else i - 2) for i in range(devices)]
    pair = [(i, i ^ 1) for i in range(devices)]
    block = lax.axis_index("seq").astype(jnp.int32)
    upper = lax.rem(block, 4) >= 2
    odd = lax.rem(block, 2) == 1
    flags = jnp.stack([block, upper.astype(jnp.int32), odd.astype(jnp.int32)])
    block = block.reshape(1)

    bounds = [0]
    for heads in CHUNKS:
        bounds.append(bounds[-1] + heads)
    assert bounds[-1] == KEY_VALUE_HEADS
    own = []
    for first, heads in zip(bounds, CHUNKS):
        assert first % heads == 0
        own.append(pack(flags, key_rows, value_matrix, first, heads))

    def send(piece, pairs):
        return lax.ppermute(piece, "seq", pairs)

    output = None
    for chunk, heads in enumerate(CHUNKS):
        mine = own[chunk]
        distant = send(mine, far)
        middle = send(jnp.where(upper, distant, mine), swap)
        pair1 = send(jnp.where(odd, distant, mine), pair)
        pair2 = send(middle, pair)
        output = attend(
            block, queries, (mine, distant, middle, pair1, pair2), bounds[chunk], heads, output
        )
    return output


def solution(mesh):
    rows = P(("groups", "seq"), None)
    return jax.shard_map(
        per_device, mesh=mesh, in_specs=(rows, rows, rows), out_specs=rows, check_vma=False
    )
```

```python
import jax
import jax.numpy as jnp
from jax import lax
from jax.experimental import pallas as pl
from jax.experimental.pallas import tpu as pltpu
from jax.sharding import PartitionSpec as P


QUERY_HEADS = 32
KEY_VALUE_HEADS = 16
HEAD_WIDTH = 128
WINDOW = 1024
GROUP = QUERY_HEADS // KEY_VALUE_HEADS

score_scale = 168.0 ** (-0.5)
LOG2_E = 1.4426950408889634
masked_value = -1e30
CHUNKS = (2, 2, 2, 2, 2, 2, 2, 2)


def pack_kernel(key_ref, value_ref, out_ref):
    length = key_ref.shape[0]
    for head in range(out_ref.shape[0]):
        columns = slice(head * HEAD_WIDTH, (head + 1) * HEAD_WIDTH)
        out_ref[head, :length] = key_ref[:, columns]
        for start in range(0, length, HEAD_WIDTH):
            rows = slice(length + start, length + start + HEAD_WIDTH)
            out_ref[head, rows] = value_ref[start : start + HEAD_WIDTH, columns].T


def pack(key_rows, value_matrix, first, heads):
    length = key_rows.shape[0]
    spec = pl.BlockSpec((length, heads * HEAD_WIDTH), lambda _: (0, first // heads))
    return pl.pallas_call(
        pack_kernel,
        out_shape=jax.ShapeDtypeStruct((heads, 2 * length, HEAD_WIDTH), key_rows.dtype),
        grid=(1,),
        in_specs=[spec, spec],
        out_specs=pl.BlockSpec((heads, 2 * length, HEAD_WIDTH), lambda _: (0, 0, 0)),
        compiler_params=pltpu.CompilerParams(vmem_limit_bytes=8 << 20),
        cost_estimate=pl.CostEstimate(
            flops=0, transcendentals=0, bytes_accessed=8 * heads * length * HEAD_WIDTH
        ),
    )(key_rows, value_matrix)


def attend_kernel(q_ref, own_ref, far_ref, mid_ref, pair1_ref, pair2_ref, *rest):
    o_ref, *score_refs = rest[-5:-2]
    max_refs = rest[-2:]
    heads, length = own_ref.shape[0], q_ref.shape[0]
    block = lax.axis_index("seq")
    odd = lax.rem(block, 2)

    def bias_of(back):
        return jnp.where(block >= back, 0.0, masked_value).astype(jnp.float32)

    far_bias = bias_of(4)
    biases = (0.0, bias_of(2), bias_of(3 - 2 * odd), bias_of(1 + 2 * odd))
    others = (None, mid_ref, pair1_ref, pair2_ref)
    across = (((1,), (1,)), ((), ()))
    scale = score_scale * LOG2_E
    ones = jnp.ones((16, length), jnp.bfloat16)
    key_pos = lax.broadcasted_iota(jnp.int32, (length, length), 0)
    query_pos = lax.broadcasted_iota(jnp.int32, (length, length), 1)
    causal = key_pos <= query_pos

    def columns(head, g):
        return pl.ds(pl.multiple_of((head * GROUP + g) * HEAD_WIDTH, HEAD_WIDTH), HEAD_WIDTH)

    def score(head, g, part, row_max):
        query = q_ref[:, columns(head, g)]

        def product(ref):
            return lax.dot_general(
                ref[head, :length], query, across, preferred_element_type=jnp.float32
            )

        if part == 0:
            raw = jnp.where(causal, product(own_ref), product(far_ref) + far_bias)
        else:
            raw = product(others[part])
        score_refs[g][part * length : (part + 1) * length] = raw
        largest = jnp.max(raw.reshape(length // 8, 8, length), axis=0) + biases[part]
        return largest if row_max is None else jnp.maximum(row_max, largest)

    def keep_max(g, row_max):
        row_max = jnp.max(row_max, axis=0, keepdims=True) * scale
        max_refs[g][...] = jnp.broadcast_to(row_max, max_refs[g].shape)

    def weigh(head, g, part, total):
        shift = max_refs[g][0:1] - biases[part] * scale
        weights = jnp.exp2(score_refs[g][part * length : (part + 1) * length] * scale - shift)
        if part == 0:
            pieces = (
                (own_ref, jnp.where(causal, weights, 0.0)),
                (far_ref, jnp.where(causal, 0.0, weights)),
            )
        else:
            pieces = ((others[part], weights),)
        for ref, piece in pieces:
            values = jnp.concatenate(
                [
                    ref[head, length + start : length + start + HEAD_WIDTH]
                    for start in range(0, length, HEAD_WIDTH)
                ],
                axis=1,
            )
            product = jnp.dot(
                jnp.concatenate([values, ones], axis=0),
                piece.astype(jnp.bfloat16),
                preferred_element_type=jnp.float32,
            )
            total = product if total is None else total + product
        return total

    def finish(head, g, total):
        result = total[:HEAD_WIDTH] / total[HEAD_WIDTH : HEAD_WIDTH + 1]
        o_ref[:, columns(head, g)] = result.T.astype(o_ref.dtype)

    def overlap(head, g, next_head, next_g):
        row_max = total = None
        for part in range(4):
            row_max = score(next_head, next_g, part, row_max)
            total = weigh(head, g, part, total)
        keep_max(next_g, row_max)
        finish(head, g, total)

    row_max = None
    for part in range(4):
        row_max = score(0, 0, part, row_max)
    keep_max(0, row_max)

    def step(head, _):
        overlap(head, 0, head, 1)
        overlap(head, 1, jnp.minimum(head + 1, heads - 1), 0)
        return 0

    lax.fori_loop(0, heads, step, 0)


def attend(queries, pieces, first, heads, output):
    length = queries.shape[0]
    kv_spec = pl.BlockSpec((heads, 2 * length, HEAD_WIDTH), lambda _: (0, 0, 0))
    q_spec = pl.BlockSpec((length, heads * GROUP * HEAD_WIDTH), lambda _: (0, first // heads))
    specs = [q_spec] + [kv_spec] * len(pieces)
    args = [queries, *pieces]
    aliases = {}
    if output is not None:
        aliases = {len(args): 0}
        specs.append(pl.BlockSpec(memory_space=pl.ANY))
        args.append(output)
    keys = len(pieces) * length
    return pl.pallas_call(
        attend_kernel,
        out_shape=jax.ShapeDtypeStruct(queries.shape, queries.dtype),
        grid=(1,),
        in_specs=specs,
        out_specs=q_spec,
        scratch_shapes=[pltpu.VMEM((WINDOW, length), jnp.float32)] * 2
        + [pltpu.VMEM((8, length), jnp.float32)] * 2,
        input_output_aliases=aliases,
        compiler_params=pltpu.CompilerParams(vmem_limit_bytes=16 << 20),
        cost_estimate=pl.CostEstimate(
            flops=heads * GROUP * length * keys * HEAD_WIDTH * 4,
            transcendentals=heads * GROUP * length * WINDOW,
            bytes_accessed=heads * HEAD_WIDTH * length * 2 * (2 * len(pieces) + 2 * GROUP),
        ),
    )(*args)


def per_device(queries, key_rows, value_matrix):
    length = queries.shape[0]
    devices = lax.axis_size("seq")
    assert WINDOW == 4 * length and devices % 4 == 0
    far = [(i, (i + 4) % devices) for i in range(devices)]
    swap = [(i, i + 2 if i % 4 < 2 else i - 2) for i in range(devices)]
    pair = [(i, i ^ 1) for i in range(devices)]
    block = lax.axis_index("seq").astype(jnp.int32)
    upper = lax.rem(block, 4) >= 2
    odd = lax.rem(block, 2) == 1
    key_rows, value_matrix, upper, odd = lax.optimization_barrier(
        (key_rows, value_matrix, upper, odd)
    )

    bounds = [0]
    for heads in CHUNKS:
        bounds.append(bounds[-1] + heads)
    assert bounds[-1] == KEY_VALUE_HEADS
    own = []
    for first, heads in zip(bounds, CHUNKS):
        assert first % heads == 0
        own.append(pack(key_rows, value_matrix, first, heads))

    def send(piece, pairs):
        return lax.ppermute(piece, "seq", pairs)

    output = None
    for chunk, heads in enumerate(CHUNKS):
        mine = own[chunk]
        distant = send(mine, far)
        middle = send(jnp.where(upper, distant, mine), swap)
        pair1 = send(jnp.where(odd, distant, mine), pair)
        pair2 = send(middle, pair)
        output = attend(
            queries, (mine, distant, middle, pair1, pair2), bounds[chunk], heads, output
        )
    return output


def solution(mesh):
    rows = P(("groups", "seq"), None)
    return jax.shard_map(
        per_device, mesh=mesh, in_specs=(rows, rows, rows), out_specs=rows, check_vma=False
    )
```

```python
import jax
import jax.numpy as jnp
from jax import lax
from jax.experimental import pallas as pl
from jax.experimental.pallas import tpu as pltpu
from jax.sharding import PartitionSpec as P


QUERY_HEADS = 32
KEY_VALUE_HEADS = 16
HEAD_WIDTH = 128
WINDOW = 1024
GROUP = QUERY_HEADS // KEY_VALUE_HEADS

score_scale = 168.0 ** (-0.5)
LOG2_E = 1.4426950408889634
masked_value = -1e30
CHUNKS = (2, 2, 2, 2, 2, 2, 2, 2)
UNROLL = 2


def pack_kernel(key_ref, value_ref, out_ref):
    length = key_ref.shape[0]
    for head in range(out_ref.shape[0]):
        columns = slice(head * HEAD_WIDTH, (head + 1) * HEAD_WIDTH)
        out_ref[head, :length] = key_ref[:, columns]
        for start in range(0, length, HEAD_WIDTH):
            rows = slice(length + start, length + start + HEAD_WIDTH)
            out_ref[head, rows] = value_ref[start : start + HEAD_WIDTH, columns].T


def pack(key_rows, value_matrix, first, heads):
    length = key_rows.shape[0]
    spec = pl.BlockSpec((length, heads * HEAD_WIDTH), lambda _: (0, first // heads))
    if first == 0:
        key_rows = pltpu.with_memory_space_constraint(key_rows, pltpu.HBM)
        value_matrix = pltpu.with_memory_space_constraint(value_matrix, pltpu.HBM)
    return pl.pallas_call(
        pack_kernel,
        out_shape=jax.ShapeDtypeStruct((heads, 2 * length, HEAD_WIDTH), key_rows.dtype),
        grid=(1,),
        in_specs=[spec, spec],
        out_specs=pl.BlockSpec((heads, 2 * length, HEAD_WIDTH), lambda _: (0, 0, 0)),
        compiler_params=pltpu.CompilerParams(vmem_limit_bytes=8 << 20),
        cost_estimate=pl.CostEstimate(
            flops=0, transcendentals=0, bytes_accessed=8 * heads * length * HEAD_WIDTH
        ),
    )(key_rows, value_matrix)


def attend_kernel(q_ref, own_ref, far_ref, mid_ref, pair1_ref, pair2_ref, *rest):
    o_ref, score_ref, max_ref = rest[-3:]
    heads, length = own_ref.shape[0], q_ref.shape[0]
    block = lax.axis_index("seq")
    odd = lax.rem(block, 2)

    def bias_of(back):
        return jnp.where(block >= back, 0.0, masked_value).astype(jnp.float32)

    far_bias = bias_of(4)
    biases = (0.0, bias_of(2), bias_of(3 - 2 * odd), bias_of(1 + 2 * odd))
    others = (None, mid_ref, pair1_ref, pair2_ref)
    across = (((1,), (1,)), ((), ()))
    scale = score_scale * LOG2_E
    ones = jnp.ones((16, length), jnp.bfloat16)
    key_pos = lax.broadcasted_iota(jnp.int32, (length, length), 0)
    query_pos = lax.broadcasted_iota(jnp.int32, (length, length), 1)
    causal = key_pos <= query_pos

    def columns(unit):
        return pl.ds(pl.multiple_of(unit * HEAD_WIDTH, HEAD_WIDTH), HEAD_WIDTH)

    def score(unit, part, row_max):
        head = lax.div(unit, GROUP)
        query = q_ref[:, columns(unit)]

        def product(ref):
            return lax.dot_general(
                ref[head, :length], query, across, preferred_element_type=jnp.float32
            )

        if part == 0:
            raw = jnp.where(causal, product(own_ref), product(far_ref) + far_bias)
        else:
            raw = product(others[part])
        score_ref[part * length : (part + 1) * length] = raw
        largest = jnp.max(raw.reshape(length // 8, 8, length), axis=0) + biases[part]
        return largest if row_max is None else jnp.maximum(row_max, largest)

    def keep_max(row_max):
        row_max = jnp.max(row_max, axis=0, keepdims=True) * scale
        max_ref[...] = jnp.broadcast_to(row_max, max_ref.shape)

    def weigh(unit, part, total):
        head = lax.div(unit, GROUP)
        shift = max_ref[0:1] - biases[part] * scale
        weights = jnp.exp2(score_ref[part * length : (part + 1) * length] * scale - shift)
        if part == 0:
            pieces = (
                (own_ref, jnp.where(causal, weights, 0.0)),
                (far_ref, jnp.where(causal, 0.0, weights)),
            )
        else:
            pieces = ((others[part], weights),)
        for ref, piece in pieces:
            values = jnp.concatenate(
                [
                    ref[head, length + start : length + start + HEAD_WIDTH]
                    for start in range(0, length, HEAD_WIDTH)
                ],
                axis=1,
            )
            product = jnp.dot(
                jnp.concatenate([values, ones], axis=0),
                piece.astype(jnp.bfloat16),
                preferred_element_type=jnp.float32,
            )
            total = product if total is None else total + product
        return total

    row_max = None
    for part in range(4):
        row_max = score(0, part, row_max)
    keep_max(row_max)
    units = heads * GROUP

    def step(unit, _):
        row_max = total = None
        for part in range(4):
            total = weigh(unit, part, total)
            row_max = score(jnp.minimum(unit + 1, units - 1), part, row_max)
        keep_max(row_max)
        result = total[:HEAD_WIDTH] / total[HEAD_WIDTH : HEAD_WIDTH + 1]
        o_ref[:, columns(unit)] = result.T.astype(o_ref.dtype)
        return 0

    lax.fori_loop(0, units, step, 0, unroll=UNROLL)


def attend(queries, pieces, first, heads, output):
    length = queries.shape[0]
    kv_spec = pl.BlockSpec((heads, 2 * length, HEAD_WIDTH), lambda _: (0, 0, 0))
    q_spec = pl.BlockSpec((length, heads * GROUP * HEAD_WIDTH), lambda _: (0, first // heads))
    specs = [q_spec] + [kv_spec] * len(pieces)
    args = [queries, *pieces]
    aliases = {}
    if output is not None:
        aliases = {len(args): 0}
        specs.append(pl.BlockSpec(memory_space=pl.ANY))
        args.append(output)
    keys = len(pieces) * length
    return pl.pallas_call(
        attend_kernel,
        out_shape=jax.ShapeDtypeStruct(queries.shape, queries.dtype),
        grid=(1,),
        in_specs=specs,
        out_specs=q_spec,
        scratch_shapes=[
            pltpu.VMEM((WINDOW, length), jnp.float32),
            pltpu.VMEM((8, length), jnp.float32),
        ],
        input_output_aliases=aliases,
        compiler_params=pltpu.CompilerParams(vmem_limit_bytes=16 << 20),
        cost_estimate=pl.CostEstimate(
            flops=heads * GROUP * length * keys * HEAD_WIDTH * 4,
            transcendentals=heads * GROUP * length * WINDOW,
            bytes_accessed=heads * HEAD_WIDTH * length * 2 * (2 * len(pieces) + 2 * GROUP),
        ),
    )(*args)


def per_device(queries, key_rows, value_matrix):
    length = queries.shape[0]
    devices = lax.axis_size("seq")
    assert WINDOW == 4 * length and devices % 4 == 0
    far = [(i, (i + 4) % devices) for i in range(devices)]
    swap = [(i, i + 2 if i % 4 < 2 else i - 2) for i in range(devices)]
    pair = [(i, i ^ 1) for i in range(devices)]
    block = lax.axis_index("seq").astype(jnp.int32)
    upper = lax.rem(block, 4) >= 2
    odd = lax.rem(block, 2) == 1
    key_rows, value_matrix, upper, odd = lax.optimization_barrier(
        (key_rows, value_matrix, upper, odd)
    )

    bounds = [0]
    for heads in CHUNKS:
        bounds.append(bounds[-1] + heads)
    assert bounds[-1] == KEY_VALUE_HEADS
    own = []
    for first, heads in zip(bounds, CHUNKS):
        assert first % heads == 0
        own.append(pack(key_rows, value_matrix, first, heads))

    def send(piece, pairs):
        return lax.ppermute(piece, "seq", pairs)

    output = None
    for chunk, heads in enumerate(CHUNKS):
        mine = own[chunk]
        distant = send(mine, far)
        middle = send(jnp.where(upper, distant, mine), swap)
        pair1 = send(jnp.where(odd, distant, mine), pair)
        pair2 = send(middle, pair)
        output = attend(
            queries, (mine, distant, middle, pair1, pair2), bounds[chunk], heads, output
        )
    return output


def solution(mesh):
    rows = P(("groups", "seq"), None)
    return jax.shard_map(
        per_device, mesh=mesh, in_specs=(rows, rows, rows), out_specs=rows, check_vma=False
    )
```

```python
import jax
import jax.numpy as jnp
from jax import lax
from jax.experimental import pallas as pl
from jax.experimental.pallas import tpu as pltpu
from jax.sharding import PartitionSpec as P


QUERY_HEADS = 32
KEY_VALUE_HEADS = 16
HEAD_WIDTH = 128
WINDOW = 1024
GROUP = QUERY_HEADS // KEY_VALUE_HEADS

score_scale = 168.0 ** (-0.5)
LOG2_E = 1.4426950408889634
masked_value = -1e30
CHUNKS = (2, 2, 2, 2, 2, 2, 2, 2)
UNROLL = 2


def pack_kernel(key_ref, value_ref, out_ref):
    length = key_ref.shape[0]
    for head in range(out_ref.shape[0]):
        columns = slice(head * HEAD_WIDTH, (head + 1) * HEAD_WIDTH)
        out_ref[head, :length] = key_ref[:, columns]
        for start in range(0, length, HEAD_WIDTH):
            rows = slice(length + start, length + start + HEAD_WIDTH)
            out_ref[head, rows] = value_ref[start : start + HEAD_WIDTH, columns].T


def pack(key_rows, value_matrix, first, heads):
    length = key_rows.shape[0]
    spec = pl.BlockSpec((length, heads * HEAD_WIDTH), lambda _: (0, first // heads))
    if first == 0:
        key_rows = pltpu.with_memory_space_constraint(key_rows, pltpu.HBM)
        value_matrix = pltpu.with_memory_space_constraint(value_matrix, pltpu.HBM)
    return pl.pallas_call(
        pack_kernel,
        out_shape=jax.ShapeDtypeStruct((heads, 2 * length, HEAD_WIDTH), key_rows.dtype),
        grid=(1,),
        in_specs=[spec, spec],
        out_specs=pl.BlockSpec((heads, 2 * length, HEAD_WIDTH), lambda _: (0, 0, 0)),
        compiler_params=pltpu.CompilerParams(vmem_limit_bytes=8 << 20),
        cost_estimate=pl.CostEstimate(
            flops=0, transcendentals=0, bytes_accessed=8 * heads * length * HEAD_WIDTH
        ),
    )(key_rows, value_matrix)


def attend_kernel(q_ref, own_ref, far_ref, mid_ref, pair1_ref, pair2_ref, *rest):
    o_ref, score_ref, max_ref = rest[-3:]
    heads, length = own_ref.shape[0], q_ref.shape[0]
    block = lax.axis_index("seq")
    odd = lax.rem(block, 2)

    def bias_of(back):
        return jnp.where(block >= back, 0.0, masked_value).astype(jnp.float32)

    far_bias = bias_of(4)
    biases = (0.0, bias_of(2), bias_of(3 - 2 * odd), bias_of(1 + 2 * odd))
    others = (None, mid_ref, pair1_ref, pair2_ref)
    across = (((1,), (1,)), ((), ()))
    scale = score_scale * LOG2_E
    ones = jnp.ones((16, length), jnp.bfloat16)
    key_pos = lax.broadcasted_iota(jnp.int32, (length, length), 0)
    query_pos = lax.broadcasted_iota(jnp.int32, (length, length), 1)
    causal = key_pos <= query_pos

    def columns(unit):
        return pl.ds(pl.multiple_of(unit * HEAD_WIDTH, HEAD_WIDTH), HEAD_WIDTH)

    def score(unit, part, row_max):
        head = lax.div(unit, GROUP)
        query = q_ref[:, columns(unit)]

        def product(ref):
            return lax.dot_general(
                ref[head, :length], query, across, preferred_element_type=jnp.float32
            )

        if part == 0:
            raw = jnp.where(causal, product(own_ref), product(far_ref) + far_bias)
        else:
            raw = product(others[part])
        score_ref[part * length : (part + 1) * length] = raw
        largest = jnp.max(raw.reshape(length // 8, 8, length), axis=0) + biases[part]
        return largest if row_max is None else jnp.maximum(row_max, largest)

    def keep_max(row_max):
        row_max = jnp.max(row_max, axis=0, keepdims=True) * scale
        max_ref[...] = jnp.broadcast_to(row_max, max_ref.shape)

    def weigh(unit, part, total):
        head = lax.div(unit, GROUP)
        shift = max_ref[0:1] - biases[part] * scale
        weights = jnp.exp2(score_ref[part * length : (part + 1) * length] * scale - shift)
        if part == 0:
            pieces = (
                (own_ref, jnp.where(causal, weights, 0.0)),
                (far_ref, jnp.where(causal, 0.0, weights)),
            )
        else:
            pieces = ((others[part], weights),)
        for ref, piece in pieces:
            values = jnp.concatenate(
                [
                    ref[head, length + start : length + start + HEAD_WIDTH]
                    for start in range(0, length, HEAD_WIDTH)
                ],
                axis=1,
            )
            product = jnp.dot(
                jnp.concatenate([values, ones], axis=0),
                piece.astype(jnp.bfloat16),
                preferred_element_type=jnp.float32,
            )
            total = product if total is None else total + product
        return total

    row_max = None
    for part in range(4):
        row_max = score(0, part, row_max)
    keep_max(row_max)
    units = heads * GROUP

    def step(unit, _):
        row_max = total = None
        for part in range(4):
            total = weigh(unit, part, total)
            row_max = score(jnp.minimum(unit + 1, units - 1), part, row_max)
        keep_max(row_max)
        result = total[:HEAD_WIDTH] / total[HEAD_WIDTH : HEAD_WIDTH + 1]
        o_ref[:, columns(unit)] = result.T.astype(o_ref.dtype)
        return 0

    lax.fori_loop(0, units, step, 0, unroll=UNROLL)


def attend(queries, pieces, first, heads, output):
    length = queries.shape[0]
    kv_spec = pl.BlockSpec((heads, 2 * length, HEAD_WIDTH), lambda _: (0, 0, 0))
    q_spec = pl.BlockSpec((length, heads * GROUP * HEAD_WIDTH), lambda _: (0, first // heads))
    specs = [q_spec] + [kv_spec] * len(pieces)
    args = [queries, *pieces]
    aliases = {}
    if output is not None:
        aliases = {len(args): 0}
        specs.append(pl.BlockSpec(memory_space=pl.ANY))
        args.append(output)
    keys = len(pieces) * length
    return pl.pallas_call(
        attend_kernel,
        out_shape=jax.ShapeDtypeStruct(queries.shape, queries.dtype),
        grid=(1,),
        in_specs=specs,
        out_specs=q_spec,
        scratch_shapes=[
            pltpu.VMEM((WINDOW, length), jnp.float32),
            pltpu.VMEM((8, length), jnp.float32),
        ],
        input_output_aliases=aliases,
        compiler_params=pltpu.CompilerParams(vmem_limit_bytes=16 << 20),
        cost_estimate=pl.CostEstimate(
            flops=heads * GROUP * length * keys * HEAD_WIDTH * 4,
            transcendentals=heads * GROUP * length * WINDOW,
            bytes_accessed=heads * HEAD_WIDTH * length * 2 * (2 * len(pieces) + 2 * GROUP),
        ),
    )(*args)


def per_device(queries, key_rows, value_matrix):
    length = queries.shape[0]
    devices = lax.axis_size("seq")
    assert WINDOW == 4 * length and devices % 4 == 0
    ring = [(i, (i + 4) % devices) for i in range(devices)]
    chain = ring[:-4]
    swap = [(i, i + 2 if i % 4 < 2 else i - 2) for i in range(devices)]
    pair = [(i, i ^ 1) for i in range(devices)]
    block = lax.axis_index("seq").astype(jnp.int32)
    upper = lax.rem(block, 4) >= 2
    odd = lax.rem(block, 2) == 1
    key_rows, value_matrix, upper, odd = lax.optimization_barrier(
        (key_rows, value_matrix, upper, odd)
    )

    bounds = [0]
    for heads in CHUNKS:
        bounds.append(bounds[-1] + heads)
    assert bounds[-1] == KEY_VALUE_HEADS
    own = []
    for first, heads in zip(bounds, CHUNKS):
        assert first % heads == 0
        own.append(pack(key_rows, value_matrix, first, heads))

    def send(piece, pairs):
        return lax.ppermute(piece, "seq", pairs)

    output = None
    for chunk, heads in enumerate(CHUNKS):
        mine = own[chunk]
        distant = send(mine, ring if chunk else chain)
        middle = send(jnp.where(upper, distant, mine), swap)
        pair1 = send(jnp.where(odd, distant, mine), pair)
        pair2 = send(middle, pair)
        output = attend(
            queries, (mine, distant, middle, pair1, pair2), bounds[chunk], heads, output
        )
    return output


def solution(mesh):
    rows = P(("groups", "seq"), None)
    return jax.shard_map(
        per_device, mesh=mesh, in_specs=(rows, rows, rows), out_specs=rows, check_vma=False
    )
```

```python
import functools

import jax
import jax.numpy as jnp
from jax import lax
from jax.experimental import pallas as pl
from jax.experimental.pallas import tpu as pltpu
from jax.sharding import PartitionSpec as P


QUERY_HEADS = 32
KEY_VALUE_HEADS = 16
HEAD_WIDTH = 128
WINDOW = 1024
GROUP = QUERY_HEADS // KEY_VALUE_HEADS

score_scale = 168.0 ** (-0.5)
LOG2_E = 1.4426950408889634
masked_value = -1e30
CHUNKS = (2, 2, 2, 2, 2, 2, 2, 2)
UNROLL = 2


def pack_kernel(key_ref, value_ref, out_ref):
    length = key_ref.shape[0]
    for head in range(out_ref.shape[0]):
        columns = slice(head * HEAD_WIDTH, (head + 1) * HEAD_WIDTH)
        out_ref[head, :length] = key_ref[:, columns]
        for start in range(0, length, HEAD_WIDTH):
            rows = slice(length + start, length + start + HEAD_WIDTH)
            out_ref[head, rows] = value_ref[start : start + HEAD_WIDTH, columns].T


def pack(key_rows, value_matrix, first, heads):
    length = key_rows.shape[0]
    spec = pl.BlockSpec((length, heads * HEAD_WIDTH), lambda _: (0, first // heads))
    if first == 0:
        key_rows = pltpu.with_memory_space_constraint(key_rows, pltpu.HBM)
        value_matrix = pltpu.with_memory_space_constraint(value_matrix, pltpu.HBM)
    return pl.pallas_call(
        pack_kernel,
        out_shape=jax.ShapeDtypeStruct((heads, 2 * length, HEAD_WIDTH), key_rows.dtype),
        grid=(1,),
        in_specs=[spec, spec],
        out_specs=pl.BlockSpec((heads, 2 * length, HEAD_WIDTH), lambda _: (0, 0, 0)),
        compiler_params=pltpu.CompilerParams(vmem_limit_bytes=8 << 20),
        cost_estimate=pl.CostEstimate(
            flops=0, transcendentals=0, bytes_accessed=8 * heads * length * HEAD_WIDTH
        ),
    )(key_rows, value_matrix)


def attend_kernel(parts, early, late, q_ref, *rest):
    rest = list(rest)
    own_ref, far_ref = (rest.pop(0), rest.pop(0)) if 0 in parts else (None, None)
    others = {part: rest.pop(0) for part in parts if part}
    if late:
        before_ref, before_max_ref = rest.pop(0), rest.pop(0)
    score_ref, max_ref = rest[-2:]
    if early:
        total_ref, total_max_ref = rest[-4:-2]
    else:
        o_ref = rest[-3]
    kv_ref = others[parts[-1]]
    heads, length = kv_ref.shape[0], q_ref.shape[0]
    block = lax.axis_index("seq")
    odd = lax.rem(block, 2)

    def bias_of(back):
        return jnp.where(block >= back, 0.0, masked_value).astype(jnp.float32)

    far_bias = bias_of(4)
    biases = (0.0, bias_of(2), bias_of(3 - 2 * odd), bias_of(1 + 2 * odd))
    across = (((1,), (1,)), ((), ()))
    scale = score_scale * LOG2_E
    ones = jnp.ones((16, length), jnp.bfloat16)
    key_pos = lax.broadcasted_iota(jnp.int32, (length, length), 0)
    query_pos = lax.broadcasted_iota(jnp.int32, (length, length), 1)
    causal = key_pos <= query_pos

    def columns(unit):
        return pl.ds(pl.multiple_of(unit * HEAD_WIDTH, HEAD_WIDTH), HEAD_WIDTH)

    def score(unit, part, row_max):
        head = lax.div(unit, GROUP)
        query = q_ref[:, columns(unit)]

        def product(ref):
            return lax.dot_general(
                ref[head, :length], query, across, preferred_element_type=jnp.float32
            )

        if part == 0:
            raw = jnp.where(causal, product(own_ref), product(far_ref) + far_bias)
        else:
            raw = product(others[part])
        slot = parts.index(part) * length
        score_ref[slot : slot + length] = raw
        largest = jnp.max(raw.reshape(length // 8, 8, length), axis=0) + biases[part]
        return largest if row_max is None else jnp.maximum(row_max, largest)

    def keep_max(unit, row_max):
        row_max = jnp.max(row_max, axis=0, keepdims=True) * scale
        row_max = jnp.broadcast_to(row_max, max_ref.shape)
        max_ref[...] = jnp.maximum(row_max, before_max_ref[unit]) if late else row_max

    def weigh(unit, part, total):
        head = lax.div(unit, GROUP)
        shift = max_ref[0:1] - biases[part] * scale
        slot = parts.index(part) * length
        weights = jnp.exp2(score_ref[slot : slot + length] * scale - shift)
        if part == 0:
            pieces = (
                (own_ref, jnp.where(causal, weights, 0.0)),
                (far_ref, jnp.where(causal, 0.0, weights)),
            )
        else:
            pieces = ((others[part], weights),)
        for ref, piece in pieces:
            values = jnp.concatenate(
                [
                    ref[head, length + start : length + start + HEAD_WIDTH]
                    for start in range(0, length, HEAD_WIDTH)
                ],
                axis=1,
            )
            product = jnp.dot(
                jnp.concatenate([values, ones], axis=0),
                piece.astype(jnp.bfloat16),
                preferred_element_type=jnp.float32,
            )
            total = product if total is None else total + product
        return total

    row_max = None
    for part in parts:
        row_max = score(0, part, row_max)
    keep_max(0, row_max)
    units = heads * GROUP

    def step(unit, _):
        row_max = total = None
        if late:
            total = before_ref[unit] * jnp.exp2(before_max_ref[unit, 0:1] - max_ref[0:1])
        if early:
            total_max_ref[unit] = max_ref[...]
        following = jnp.minimum(unit + 1, units - 1)
        for part in parts:
            total = weigh(unit, part, total)
            row_max = score(following, part, row_max)
        keep_max(following, row_max)
        if early:
            total_ref[unit] = total
        else:
            result = total[:HEAD_WIDTH] / total[HEAD_WIDTH : HEAD_WIDTH + 1]
            o_ref[:, columns(unit)] = result.T.astype(o_ref.dtype)
        return 0

    lax.fori_loop(0, units, step, 0, unroll=UNROLL if len(parts) == 4 else units)


def attend(queries, pieces, first, heads, output, parts=(0, 1, 2, 3), early=False, before=()):
    length = queries.shape[0]
    units = heads * GROUP
    sums = (units, HEAD_WIDTH + 16, length)
    maxima = (units, 8, length)

    def whole(shape):
        return pl.BlockSpec(shape, lambda _: (0,) * len(shape))

    q_spec = pl.BlockSpec((length, units * HEAD_WIDTH), lambda _: (0, first // heads))
    args = [queries, *pieces, *before]
    specs = [q_spec] + [whole(arg.shape) for arg in args[1:]]
    aliases = {}
    if output is not None:
        aliases = {len(args): 0}
        specs.append(pl.BlockSpec(memory_space=pl.ANY))
        args.append(output)
    out_shape = jax.ShapeDtypeStruct(queries.shape, queries.dtype)
    out_specs = q_spec
    if early:
        out_shape = tuple(jax.ShapeDtypeStruct(shape, jnp.float32) for shape in (sums, maxima))
        out_specs = tuple(whole(shape) for shape in (sums, maxima))
    keys = len(pieces) * length
    return pl.pallas_call(
        functools.partial(attend_kernel, parts, early, bool(before)),
        out_shape=out_shape,
        grid=(1,),
        in_specs=specs,
        out_specs=out_specs,
        scratch_shapes=[
            pltpu.VMEM((len(parts) * length, length), jnp.float32),
            pltpu.VMEM((8, length), jnp.float32),
        ],
        input_output_aliases=aliases,
        compiler_params=pltpu.CompilerParams(vmem_limit_bytes=16 << 20),
        cost_estimate=pl.CostEstimate(
            flops=units * length * keys * HEAD_WIDTH * 4,
            transcendentals=units * length * len(parts) * length,
            bytes_accessed=heads * HEAD_WIDTH * length * 2 * (2 * len(pieces) + 2 * GROUP),
        ),
    )(*args)


def per_device(queries, key_rows, value_matrix):
    length = queries.shape[0]
    devices = lax.axis_size("seq")
    assert WINDOW == 4 * length and devices % 4 == 0
    ring = [(i, (i + 4) % devices) for i in range(devices)]
    chain = ring[:-4]
    swap = [(i, i + 2 if i % 4 < 2 else i - 2) for i in range(devices)]
    pair = [(i, i ^ 1) for i in range(devices)]
    block = lax.axis_index("seq").astype(jnp.int32)
    upper = lax.rem(block, 4) >= 2
    odd = lax.rem(block, 2) == 1
    key_rows, value_matrix, upper, odd = lax.optimization_barrier(
        (key_rows, value_matrix, upper, odd)
    )

    bounds = [0]
    for heads in CHUNKS:
        bounds.append(bounds[-1] + heads)
    assert bounds[-1] == KEY_VALUE_HEADS
    own = []
    for first, heads in zip(bounds, CHUNKS):
        assert first % heads == 0
        own.append(pack(key_rows, value_matrix, first, heads))

    def send(piece, pairs):
        return lax.ppermute(piece, "seq", pairs)

    output = None
    for chunk, heads in enumerate(CHUNKS):
        mine = own[chunk]
        distant = send(mine, ring if chunk else chain)
        middle = send(jnp.where(upper, distant, mine), swap)
        pair1 = send(jnp.where(odd, distant, mine), pair)
        pair2 = send(middle, pair)
        first = bounds[chunk]
        pieces = (mine, distant, middle, pair1, pair2)
        options = {}
        if chunk == len(CHUNKS) - 1:
            before = attend(
                queries, (mine, distant, pair1), first, heads, None, parts=(0, 2), early=True
            )
            before = attend(
                queries, (middle,), first, heads, None, parts=(1,), early=True, before=before
            )
            pieces = (pair2,)
            options = {"parts": (3,), "before": before}
        output = attend(queries, pieces, first, heads, output, **options)
    return output


def solution(mesh):
    rows = P(("groups", "seq"), None)
    return jax.shard_map(
        per_device, mesh=mesh, in_specs=(rows, rows, rows), out_specs=rows, check_vma=False
    )
```

```python
import functools

import jax
import jax.numpy as jnp
from jax import lax
from jax.experimental import pallas as pl
from jax.experimental.pallas import tpu as pltpu
from jax.sharding import PartitionSpec as P


QUERY_HEADS = 32
KEY_VALUE_HEADS = 16
HEAD_WIDTH = 128
WINDOW = 1024
GROUP = QUERY_HEADS // KEY_VALUE_HEADS

score_scale = 168.0 ** (-0.5)
LOG2_E = 1.4426950408889634
masked_value = -1e30
CHUNKS = (2, 2, 2, 2, 2, 2, 2, 2)
UNROLL = 2


def pack_kernel(key_ref, value_ref, out_ref):
    length = key_ref.shape[0]
    for head in range(out_ref.shape[0]):
        columns = slice(head * HEAD_WIDTH, (head + 1) * HEAD_WIDTH)
        out_ref[head, :length] = key_ref[:, columns]
        for start in range(0, length, HEAD_WIDTH):
            rows = slice(length + start, length + start + HEAD_WIDTH)
            out_ref[head, rows] = value_ref[start : start + HEAD_WIDTH, columns].T


def pack(key_rows, value_matrix, first, heads):
    length = key_rows.shape[0]
    spec = pl.BlockSpec((length, heads * HEAD_WIDTH), lambda _: (0, first // heads))
    if first == 0:
        key_rows = pltpu.with_memory_space_constraint(key_rows, pltpu.HBM)
        value_matrix = pltpu.with_memory_space_constraint(value_matrix, pltpu.HBM)
    return pl.pallas_call(
        pack_kernel,
        out_shape=jax.ShapeDtypeStruct((heads, 2 * length, HEAD_WIDTH), key_rows.dtype),
        grid=(1,),
        in_specs=[spec, spec],
        out_specs=pl.BlockSpec((heads, 2 * length, HEAD_WIDTH), lambda _: (0, 0, 0)),
        compiler_params=pltpu.CompilerParams(vmem_limit_bytes=8 << 20),
        cost_estimate=pl.CostEstimate(
            flops=0, transcendentals=0, bytes_accessed=8 * heads * length * HEAD_WIDTH
        ),
    )(key_rows, value_matrix)


def attend_kernel(parts, early, late, q_ref, *rest):
    rest = list(rest)
    own_ref, far_ref = (rest.pop(0), rest.pop(0)) if 0 in parts else (None, None)
    others = {part: rest.pop(0) for part in parts if part}
    if late:
        before_ref, before_max_ref = rest.pop(0), rest.pop(0)
    score_ref, max_ref = rest[-2:]
    if early:
        total_ref, total_max_ref = rest[-4:-2]
    else:
        o_ref = rest[-3]
    kv_ref = others[parts[-1]]
    heads, length = kv_ref.shape[0], q_ref.shape[0]
    block = lax.axis_index("seq")
    odd = lax.rem(block, 2)

    def bias_of(back):
        return jnp.where(block >= back, 0.0, masked_value).astype(jnp.float32)

    far_bias = bias_of(4)
    biases = (0.0, bias_of(2), bias_of(3 - 2 * odd), bias_of(1 + 2 * odd))
    across = (((1,), (1,)), ((), ()))
    scale = score_scale * LOG2_E
    ones = jnp.ones((16, length), jnp.bfloat16)
    key_pos = lax.broadcasted_iota(jnp.int32, (length, length), 0)
    query_pos = lax.broadcasted_iota(jnp.int32, (length, length), 1)
    causal = key_pos <= query_pos

    def columns(unit):
        return pl.ds(pl.multiple_of(unit * HEAD_WIDTH, HEAD_WIDTH), HEAD_WIDTH)

    def score(unit, part, row_max):
        head = lax.div(unit, GROUP)
        query = q_ref[:, columns(unit)]

        def product(ref):
            return lax.dot_general(
                ref[head, :length], query, across, preferred_element_type=jnp.float32
            )

        if part == 0:
            raw = jnp.where(causal, product(own_ref), product(far_ref) + far_bias)
        else:
            raw = product(others[part])
        slot = parts.index(part) * length
        score_ref[slot : slot + length] = raw
        largest = jnp.max(raw.reshape(length // 8, 8, length), axis=0) + biases[part]
        return largest if row_max is None else jnp.maximum(row_max, largest)

    def keep_max(unit, row_max):
        row_max = jnp.max(row_max, axis=0, keepdims=True) * scale
        row_max = jnp.broadcast_to(row_max, max_ref.shape)
        max_ref[...] = jnp.maximum(row_max, before_max_ref[unit]) if late else row_max

    def weigh(unit, part, total):
        head = lax.div(unit, GROUP)
        shift = max_ref[0:1] - biases[part] * scale
        slot = parts.index(part) * length
        weights = jnp.exp2(score_ref[slot : slot + length] * scale - shift)
        if part == 0:
            pieces = (
                (own_ref, jnp.where(causal, weights, 0.0)),
                (far_ref, jnp.where(causal, 0.0, weights)),
            )
        else:
            pieces = ((others[part], weights),)
        for ref, piece in pieces:
            values = jnp.concatenate(
                [
                    ref[head, length + start : length + start + HEAD_WIDTH]
                    for start in range(0, length, HEAD_WIDTH)
                ],
                axis=1,
            )
            product = jnp.dot(
                jnp.concatenate([values, ones], axis=0),
                piece.astype(jnp.bfloat16),
                preferred_element_type=jnp.float32,
            )
            total = product if total is None else total + product
        return total

    row_max = None
    for part in parts:
        row_max = score(0, part, row_max)
    keep_max(0, row_max)
    units = heads * GROUP

    def step(unit, _):
        row_max = total = None
        if late:
            total = before_ref[unit] * jnp.exp2(before_max_ref[unit, 0:1] - max_ref[0:1])
        if early:
            total_max_ref[unit] = max_ref[...]
        following = jnp.minimum(unit + 1, units - 1)
        for part in parts:
            total = weigh(unit, part, total)
            row_max = score(following, part, row_max)
        keep_max(following, row_max)
        if early:
            total_ref[unit] = total
        else:
            result = total[:HEAD_WIDTH] / total[HEAD_WIDTH : HEAD_WIDTH + 1]
            o_ref[:, columns(unit)] = result.T.astype(o_ref.dtype)
        return 0

    lax.fori_loop(0, units, step, 0, unroll=UNROLL if len(parts) == 4 else units)


def attend(queries, pieces, first, heads, output, parts=(0, 1, 2, 3), early=False, before=()):
    length = queries.shape[0]
    units = heads * GROUP
    sums = (units, HEAD_WIDTH + 16, length)
    maxima = (units, 8, length)

    def whole(shape):
        return pl.BlockSpec(shape, lambda _: (0,) * len(shape))

    q_spec = pl.BlockSpec((length, units * HEAD_WIDTH), lambda _: (0, first // heads))
    args = [queries, *pieces, *before]
    specs = [q_spec] + [whole(arg.shape) for arg in args[1:]]
    aliases = {}
    if output is not None:
        aliases = {len(args): 0}
        specs.append(pl.BlockSpec(memory_space=pl.ANY))
        args.append(output)
    out_shape = jax.ShapeDtypeStruct(queries.shape, queries.dtype)
    out_specs = q_spec
    if early:
        out_shape = tuple(jax.ShapeDtypeStruct(shape, jnp.float32) for shape in (sums, maxima))
        out_specs = tuple(whole(shape) for shape in (sums, maxima))
    keys = len(pieces) * length
    return pl.pallas_call(
        functools.partial(attend_kernel, parts, early, bool(before)),
        out_shape=out_shape,
        grid=(1,),
        in_specs=specs,
        out_specs=out_specs,
        scratch_shapes=[
            pltpu.VMEM((len(parts) * length, length), jnp.float32),
            pltpu.VMEM((8, length), jnp.float32),
        ],
        input_output_aliases=aliases,
        compiler_params=pltpu.CompilerParams(vmem_limit_bytes=16 << 20),
        cost_estimate=pl.CostEstimate(
            flops=units * length * keys * HEAD_WIDTH * 4,
            transcendentals=units * length * len(parts) * length,
            bytes_accessed=heads * HEAD_WIDTH * length * 2 * (2 * len(pieces) + 2 * GROUP),
        ),
    )(*args)


def per_device(queries, key_rows, value_matrix):
    length = queries.shape[0]
    devices = lax.axis_size("seq")
    assert WINDOW == 4 * length and devices % 4 == 0
    ring = [(i, (i + 4) % devices) for i in range(devices)]
    chain = ring[:-4]
    swap = [(i, i + 2 if i % 4 < 2 else i - 2) for i in range(devices)]
    pair = [(i, i ^ 1) for i in range(devices)]
    block = lax.axis_index("seq").astype(jnp.int32)
    upper = lax.rem(block, 4) >= 2
    odd = lax.rem(block, 2) == 1
    key_rows, value_matrix, upper, odd = lax.optimization_barrier(
        (key_rows, value_matrix, upper, odd)
    )

    bounds = [0]
    for heads in CHUNKS:
        bounds.append(bounds[-1] + heads)
    assert bounds[-1] == KEY_VALUE_HEADS
    own = []
    for first, heads in zip(bounds, CHUNKS):
        assert first % heads == 0
        own.append(pack(key_rows, value_matrix, first, heads))

    def send(piece, pairs):
        return lax.ppermute(piece, "seq", pairs)

    output = None
    for chunk, heads in enumerate(CHUNKS):
        mine = own[chunk]
        distant = send(mine, ring if chunk else chain)
        middle = send(jnp.where(upper, distant, mine), swap)
        pair1 = send(jnp.where(odd, distant, mine), pair)
        pair2 = send(middle, pair)
        first = bounds[chunk]
        pieces = (mine, distant, middle, pair1, pair2)
        options = {}
        if chunk == len(CHUNKS) - 1:
            before = attend(
                queries, (mine, distant, pair1), first, heads, None, parts=(0, 2), early=True
            )
            pieces = (middle, pair2)
            options = {"parts": (1, 3), "before": before}
        output = attend(queries, pieces, first, heads, output, **options)
    return output


def solution(mesh):
    rows = P(("groups", "seq"), None)
    return jax.shard_map(
        per_device, mesh=mesh, in_specs=(rows, rows, rows), out_specs=rows, check_vma=False
    )
```
